32 devices in a mesh: groups: 2 (over y), seq: 8 (over z, x), dp: 2 (over core).
Axes of the slice: x: 2, y: 2, z: 4, core: 2. Of those that a mesh axis runs over, the one named last changes fastest.
Arguments:
- activations: bfloat16 [64, 4096], P(('groups', 'seq', 'dp')), parts along dimension 0, may hold values from -6 to 6
- grad_out: bfloat16 [64, 14336], P(('groups', 'seq', 'dp')), parts along dimension 0, may hold values from -1 to 1
- weight_regions: bfloat16 [8, 512, 14336], P('seq', 'dp'), may hold values from -0.375 to 0.375
- keep_blocks: int32 [8, 4, 112], P('seq'), may hold values from 0 to 1, as said below
Outputs:
- grad_weight: float32 [16, 512, 14336], P(('groups', 'seq'), 'dp'), parts along dimension 0
- grad_input: float32 [64, 4096], P(('groups', 'seq', 'dp')), parts along dimension 0
The draws below stay inside these ranges and needn't reach their ends.
There are 2 independent parts, one for each index of `groups`. The reference program is written for one: setup_inputs(seed, part) draws one part's arguments, and reference() takes and returns one part's arrays. A program takes and returns all parts, laid end to end along the dimension named above; an argument that names none is the same for every part. Nothing has to cross between parts.
Inputs may be any that keep to these rules, and one draw needn't show every extreme that they name: `keep_blocks`: the tile rows of each region fall into bands of 2 rows in order; a band keeps at least 56 and at most 168 of its 224 tiles, some band of some region exactly 168; where a band's kept tiles lie is random, so the kept counts of tile rows differ.
All inputs are finite; a program needn't handle non-finite values.
Results may differ from the reference program's by a relative error of at most 0.0003.
Values may be sent and summed in bfloat16 or wider, within the bound.
A program may use at most 192 MiB of HBM per device.

```python
import jax
import jax.numpy as jnp

D = 4096
FF = 14336
BLK = 128
ROWG = 8
TOKENS = 32
COLG = 1
NREG = 8
RD = 512
RF = 14336
RDB = 4
RFB = 112
BANDR = 2
HB = 224
BAND_MOST = 168


def draw_keep_blocks(key, part):
    band_total = RDB // BANDR
    fewest = HB - BAND_MOST
    key_count, key_full, key_score = jax.random.split(key, 3)
    counts = jax.random.randint(key_count, (NREG, band_total), fewest, BAND_MOST + 1)
    fullest = jax.random.randint(key_full, (), 0, NREG * band_total)
    flat_place = jnp.arange(NREG * band_total).reshape(NREG, band_total)
    counts = jnp.where(flat_place == fullest, BAND_MOST, counts)
    scores = jax.random.randint(key_score, (NREG, band_total, HB), 0, 1 << 20) * HB + jnp.arange(HB)[None, None, :]
    ranking = jnp.argsort(scores, axis=2)
    positions = jnp.argsort(ranking, axis=2)
    kept_mask = (positions < counts[:, :, None]).astype(jnp.int32)
    return kept_mask.reshape(NREG, RDB, RFB)


def block_scale(own_key, extent, pieces, smallest, top_value):
    gain, own = 1.0, jax.random.fold_in(own_key, 6)
    for axis_at, shards_of in pieces:
        heights = jnp.exp(jax.random.uniform(jax.random.fold_in(own, axis_at), (shards_of,), jnp.float32, smallest / len(pieces), top_value / len(pieces)))
        gain = gain * jnp.repeat(heights, extent[axis_at] // shards_of).reshape([-1 if axis == axis_at else 1 for axis in range(len(extent))])
    return gain


def gaussian(rng, dims, scale, most, pieces=(), kind=jnp.bfloat16):
    result = scale * jax.random.normal(rng, dims, jnp.float32)
    if pieces:
        result = result * block_scale(rng, dims, pieces, -0.22, 0.18)
    return jnp.clip(result, -most, most).astype(kind)


def setup_inputs(seed: int = 0, part: int = 0) -> dict:
    arg_keys = jax.random.split(jax.random.key(seed), 5)
    part_keys = jax.random.split(jax.random.fold_in(arg_keys[4], part), 5)
    activations = gaussian(part_keys[0], (TOKENS, D), 1.0, 6.0, ((0, 16),))
    grad_out = gaussian(part_keys[1], (TOKENS, FF), TOKENS ** -0.5, 1.0, ((0, 16),))
    weight_regions = gaussian(arg_keys[2], (NREG, RD, RF), (max(1, FF // (2 * TOKENS))) ** -0.5, 0.375, ((0, 8), (1, 2)))
    keep_blocks = draw_keep_blocks(jax.random.fold_in(arg_keys[4], 71), part)
    return {"activations": activations, "grad_out": grad_out, "weight_regions": weight_regions, "keep_blocks": keep_blocks}


def to_dense(regions):
    return regions.reshape(COLG, ROWG, RD, RF).transpose(1, 2, 0, 3).reshape(D, FF)


def to_regions(matrix):
    return matrix.reshape(ROWG, RD, COLG, RF).transpose(2, 0, 1, 3).reshape(NREG, RD, RF)


def reference(activations, grad_out, weight_regions, keep_blocks):
    keep_mask = jnp.repeat(jnp.repeat(keep_blocks, BLK, axis=1), BLK, axis=2)
    masked_weight = to_dense(weight_regions * keep_mask.astype(weight_regions.dtype))
    grad_input = jnp.dot(grad_out, masked_weight.T, preferred_element_type=jnp.float32)
    full_grad = jnp.dot(activations.T, grad_out, preferred_element_type=jnp.float32)
    grad_weight = to_regions(full_grad) * keep_mask.astype(jnp.float32)
    return grad_weight, grad_input
```

```python
import functools

import jax
import jax.numpy as jnp
from jax import lax
from jax.experimental import pallas as pl
from jax.experimental.pallas import tpu as pltpu
from jax.sharding import PartitionSpec as P

ROWG = 8
XDIM = 2
CHUNKS = 2
VMEM_A = 56 << 20
VMEM_B = 40 << 20
MESH = pl.DeviceIdType.MESH


def gather_kernel(
    zdim, sub, act, grad, weight, keep,
    mg_out, xt_out, gi_out,
    gbuf, gslot, xslot, pslot, wbuf,
    gsend, grecv, xsend, xrecv, psend, precv, wsem, lsem,
):
    seq = lax.axis_index("seq")
    core = lax.axis_index("dp")
    z, x = seq // XDIM, seq % XDIM
    slots = zdim * XDIM * 2
    rows, cols = grad.shape
    width = cols // CHUNKS
    feats = weight.shape[0]
    tile = cols // keep.shape[1]
    band_tiles = feats // tile
    zdists = range(1, zdim)

    def slot_of(dz, rx, rc):
        return (dz * XDIM + rx) * 2 + rc

    def peer(dz, rx, rc):
        pz = lax.rem(z + dz, zdim)
        px = x if rx == 0 else 1 - x
        pc = core if rc == 0 else 1 - core
        return pz * XDIM + px, pc

    def devid(dz, rx, rc):
        ps, pc = peer(dz, rx, rc)
        return {"seq": ps, "dp": pc}

    everyone = [(dz, rx, rc) for dz in range(zdim) for rx in range(XDIM) for rc in range(2)]
    others = everyone[1:]

    barrier = pltpu.get_barrier_semaphore()
    for who in others:
        pl.semaphore_signal(barrier, inc=1, device_id=devid(*who), device_id_type=MESH)

    def wcopy(q):
        c = pl.ds(q * width, width)
        return pltpu.make_async_copy(weight.at[:, c], wbuf.at[:, c], wsem.at[q])

    def own(q):
        return grad.at[:, pl.ds(q * width, width)]

    my_col = pl.multiple_of((seq * 2 + core) * feats, feats)
    xown = pltpu.make_async_copy(act.at[:, pl.ds(my_col, feats)], xslot.at[0], lsem.at[CHUNKS])
    xown.start()
    gown = [pltpu.make_async_copy(own(q), gslot.at[q, 0], lsem.at[q]) for q in range(CHUNKS)]
    for q in range(CHUNKS):
        gown[q].start()
    for q in range(CHUNKS):
        wcopy(q).start()

    pl.semaphore_wait(barrier, len(others))

    def push(q, src, to, dst_slot, sem):
        pltpu.make_async_remote_copy(
            src_ref=src, dst_ref=gslot.at[q, dst_slot],
            send_sem=gsend, recv_sem=grecv.at[q, sem],
            device_id=devid(*to), device_id_type=MESH,
        ).start()

    def arrived(q, sem, count):
        ref = gslot.at[q, pl.ds(0, count)]
        pltpu.make_async_remote_copy(
            src_ref=ref, dst_ref=ref, send_sem=gsend, recv_sem=grecv.at[q, sem],
            device_id=devid(0, 0, 1), device_id_type=MESH,
        ).wait_recv()

    for q in range(CHUNKS):
        for dz in reversed(zdists):
            push(q, own(q), (dz, 0, 0), slot_of(zdim - dz, 0, 0), zdim - dz)
        push(q, own(q), (0, 1, 0), slot_of(0, 1, 0), zdim)
        push(q, own(q), (0, 0, 1), slot_of(0, 0, 1), 0)

    def xcopy(who):
        ps, pc = peer(*who)
        dz, rx, rc = who
        dst = slot_of((zdim - dz) % zdim, rx, rc)
        col = pl.multiple_of((ps * 2 + pc) * feats, feats)
        return pltpu.make_async_remote_copy(
            src_ref=act.at[:, pl.ds(col, feats)], dst_ref=xslot.at[dst],
            send_sem=xsend, recv_sem=xrecv,
            device_id={"seq": ps, "dp": pc}, device_id_type=MESH,
        )

    for who in others:
        xcopy(who).start()

    def z_stage(q):
        for dz in zdists:
            arrived(q, dz, 1)
            slot = slot_of(dz, 0, 0)
            push(q, gslot.at[q, slot], (0, 1, 0), slot_of(dz, 1, 0), zdim + dz)
            push(q, gslot.at[q, slot], (0, 0, 1), slot_of(dz, 0, 1), 0)

    def x_stage(q):
        for dz in range(zdim):
            arrived(q, zdim + dz, 1)
            push(q, gslot.at[q, slot_of(dz, 1, 0)], (0, 0, 1), slot_of(dz, 1, 1), 0)

    def assemble(q, rc):
        for s in range(rc, slots, 2):
            gbuf[rows * s:rows * (s + 1), q * width:(q + 1) * width] = gslot[q, s]

    def compute(q, acc):
        gown[q].wait()
        assemble(q, 0)
        arrived(q, 0, slots // 2)
        assemble(q, 1)
        wcopy(q).wait()

        def step(j, acc):
            off = pl.multiple_of(q * width + j * sub, sub)
            g = gbuf[:, pl.ds(off, sub)]
            parts = []
            for a in range(band_tiles):
                pieces = []
                for t in range(sub // tile):
                    kept = keep[core * band_tiles + a, (q * width) // tile + j * (sub // tile) + t]
                    mask = jnp.full((slots * rows, tile), kept.astype(jnp.float32), jnp.float32)
                    pieces.append(g[:, t * tile:(t + 1) * tile] * mask.astype(jnp.bfloat16))
                parts.append(jnp.concatenate(pieces, axis=1))
            lhs = jnp.concatenate(parts, axis=0)
            mg_out[:, pl.ds(off, sub)] = lhs
            return acc + lax.dot_general(
                lhs, wbuf[:, pl.ds(off, sub)], (((1,), (1,)), ((), ())),
                preferred_element_type=jnp.float32,
            )

        return lax.fori_loop(0, width // sub, step, acc, unroll=True)

    acc = jnp.zeros((band_tiles * slots * rows, feats), jnp.float32)
    for t in range(CHUNKS + 2):
        if t < CHUNKS:
            z_stage(t)
        if 0 <= t - 1 < CHUNKS:
            x_stage(t - 1)
        if 0 <= t - 2 < CHUNKS:
            acc = compute(t - 2, acc)

    n = slots * rows
    for s in range(slots):
        for a in range(band_tiles):
            pslot[s, :, a * tile:(a + 1) * tile] = acc[a * n + rows * s:a * n + rows * (s + 1), a * tile:(a + 1) * tile]

    for who in others:
        dz, rx, rc = who
        pltpu.make_async_remote_copy(
            src_ref=pslot.at[slot_of(dz, rx, rc)], dst_ref=gi_out.at[:, pl.ds(my_col, feats)],
            send_sem=psend, recv_sem=precv,
            device_id=devid(*who), device_id_type=MESH,
        ).start()
    mine = pltpu.make_async_copy(pslot.at[0], gi_out.at[:, pl.ds(my_col, feats)], lsem.at[CHUNKS + 1])
    mine.start()

    def all_of(ref, send, recv):
        return pltpu.make_async_remote_copy(
            src_ref=ref, dst_ref=ref, send_sem=send, recv_sem=recv,
            device_id=devid(0, 0, 1), device_id_type=MESH,
        )

    rest = pl.ds(0, slots - 1)
    xown.wait()
    xall = all_of(xslot.at[rest], xsend, xrecv)
    xall.wait_recv()
    panel = jnp.concatenate([xslot[s].astype(jnp.float32) for s in range(slots)], axis=0)
    xt_out[...] = panel.T.astype(jnp.bfloat16)

    xall.wait_send()
    all_of(gslot.at[:, rest], gsend, gsend).wait_send()
    mine.wait()
    pall = all_of(pslot.at[rest], psend, precv)
    pall.wait_send()
    pall.wait_recv()


def weight_kernel(band_tiles, blocks, xt, mg, gi, out, gi_out, buf, sem, gsem):
    feats, cols = out.shape
    tile = feats // band_tiles
    tokens = mg.shape[0] // band_tiles
    width = cols // blocks
    step = 2 * tile if width % (2 * tile) == 0 else width
    last = pltpu.make_async_copy(gi, gi_out, gsem)
    last.start()
    x = xt[...]
    for j in range(blocks):
        for lo in range(j * width, (j + 1) * width, step):
            for a in range(band_tiles):
                buf[a * tile:(a + 1) * tile, lo:lo + step] = jnp.dot(
                    x[a * tile:(a + 1) * tile], mg[a * tokens:(a + 1) * tokens, lo:lo + step],
                    preferred_element_type=jnp.float32,
                )
        c = pl.ds(j * width, width)
        pltpu.make_async_copy(buf.at[:, c], out.at[:, c], sem).start()
    last.wait()
    pltpu.make_async_copy(buf, out, sem).wait()


def fused(activations, grad_out, weight, keep):
    rows, cols = grad_out.shape
    feats = weight.shape[0]
    zdim = lax.axis_size("seq") // XDIM
    slots = zdim * XDIM * 2
    tile = cols // keep.shape[1]
    band_tiles = feats // tile
    width = cols // CHUNKS
    sub = 8 * tile if width % (8 * tile) == 0 else tile
    hbm = pl.BlockSpec(memory_space=pltpu.HBM)
    vmem = pl.BlockSpec(memory_space=pltpu.VMEM)
    smem = pl.BlockSpec(memory_space=pltpu.SMEM)
    dma = pltpu.SemaphoreType.DMA
    mg, xt, gi = pl.pallas_call(
        functools.partial(gather_kernel, zdim, sub),
        name="gather_input_grad",
        out_shape=(
            pltpu.VMEM((band_tiles * slots * rows, cols), jnp.bfloat16),
            pltpu.VMEM((feats, slots * rows), jnp.bfloat16),
            pltpu.VMEM(activations.shape, jnp.float32),
        ),
        in_specs=[hbm, hbm, hbm, smem],
        out_specs=(vmem, vmem, vmem),
        scratch_shapes=[
            pltpu.VMEM((slots * rows, cols), jnp.bfloat16),
            pltpu.VMEM((CHUNKS, slots, rows, width), jnp.bfloat16),
            pltpu.VMEM((slots, rows, feats), jnp.bfloat16),
            pltpu.VMEM((slots, rows, feats), jnp.float32),
            pltpu.VMEM((feats, cols), jnp.bfloat16),
            dma(()),
            dma((CHUNKS, 2 * zdim)),
            dma(()),
            dma(()),
            dma(()),
            dma(()),
            dma((CHUNKS,)),
            dma((CHUNKS + 2,)),
        ],
        compiler_params=pltpu.CompilerParams(
            collective_id=0, has_side_effects=True, vmem_limit_bytes=VMEM_A
        ),
    )(activations, grad_out, weight, keep)
    blocks = 14 if (cols // tile) % 14 == 0 else 1
    gw, gi = pl.pallas_call(
        functools.partial(weight_kernel, band_tiles, blocks),
        name="weight_grad",
        out_shape=(
            jax.ShapeDtypeStruct((feats, cols), jnp.float32),
            jax.ShapeDtypeStruct(gi.shape, jnp.float32),
        ),
        in_specs=[vmem, vmem, vmem],
        out_specs=(hbm, hbm),
        scratch_shapes=[
            pltpu.VMEM((feats, cols), jnp.float32),
            dma(()),
            dma(()),
        ],
        compiler_params=pltpu.CompilerParams(vmem_limit_bytes=VMEM_B),
    )(xt, mg, gi)
    return gw[None], gi


def general(activations, grad_out, weight_regions, keep_blocks):
    tok_rows = activations.shape[0]
    seq_count = lax.axis_size("seq")
    dp_count = lax.axis_size("dp")
    col_groups = seq_count // ROWG
    band_rows = weight_regions.shape[1]
    region_cols = weight_regions.shape[2]
    region_rows = band_rows * dp_count
    core = lax.axis_index("dp")
    grad_groups = grad_out.reshape(tok_rows, col_groups, region_cols).transpose(1, 0, 2)
    grad_send = jnp.repeat(grad_groups, ROWG, axis=0)
    feature_groups = activations.reshape(tok_rows, ROWG, region_rows).transpose(1, 0, 2)
    feature_send = jnp.tile(feature_groups, (col_groups, 1, 1))
    feature_came = lax.all_to_all(feature_send, "seq", split_axis=0, concat_axis=0, tiled=True)
    grad_came = lax.all_to_all(grad_send, "seq", split_axis=0, concat_axis=0, tiled=True)
    half_rows = seq_count * tok_rows
    features = lax.all_gather(feature_came.reshape(half_rows, region_rows), "dp", axis=0, tiled=True)
    features = lax.dynamic_slice_in_dim(features, core * band_rows, band_rows, 1)
    grads = lax.all_gather(grad_came.reshape(half_rows, region_cols), "dp", axis=0, tiled=True)
    tile_rows = keep_blocks.shape[1] // dp_count
    kept = lax.dynamic_slice_in_dim(keep_blocks[0], core * tile_rows, tile_rows, 0)
    side = band_rows // tile_rows
    mask = jnp.repeat(jnp.repeat(kept, side, axis=0), side, axis=1)
    masked_weight = weight_regions[0] * mask.astype(jnp.bfloat16)
    weight_grad = lax.dot_general(
        features, grads, (((0,), (0,)), ((), ())), preferred_element_type=jnp.float32
    ) * mask.astype(jnp.float32)
    partial_value = lax.dot_general(
        grads, masked_weight, (((1,), (1,)), ((), ())), preferred_element_type=jnp.float32
    )
    bands = partial_value.reshape(dp_count, half_rows, band_rows)
    bands = lax.all_to_all(bands, "dp", split_axis=0, concat_axis=0, tiled=True)
    bands = bands.transpose(1, 0, 2).reshape(seq_count, tok_rows, region_rows)
    came = lax.all_to_all(bands, "seq", split_axis=0, concat_axis=0, tiled=True)
    summed = jnp.sum(came.reshape(col_groups, ROWG, tok_rows, region_rows), axis=0)
    return weight_grad[None], summed.transpose(1, 0, 2).reshape(tok_rows, ROWG * region_rows)


def shards(activations, grad_out, weight_regions, keep_blocks):
    if lax.axis_size("seq") == ROWG and lax.axis_size("dp") == 2:
        return fused(activations, grad_out, weight_regions[0], keep_blocks[0])
    return general(activations, grad_out, weight_regions, keep_blocks)


def solution(mesh):
    in_specs = (
        P(("groups", "seq", "dp"), None),
        P(("groups", "seq", "dp"), None),
        P("seq", "dp", None),
        P("seq", None, None),
    )
    out_specs = (P(("groups", "seq"), "dp", None), P(("groups", "seq", "dp"), None))
    return jax.shard_map(shards, mesh=mesh, in_specs=in_specs, out_specs=out_specs, check_vma=False)
```

```python
import functools

import jax
import jax.numpy as jnp
from jax import lax
from jax.experimental import pallas as pl
from jax.experimental.pallas import tpu as pltpu
from jax.sharding import PartitionSpec as P

ROWG = 8
XDIM = 2
CHUNKS = 4
LAG = 1
SUB = 7
VMEM_A = 56 << 20
VMEM_B = 40 << 20
MESH = pl.DeviceIdType.MESH


def gather_kernel(
    zdim, sub, act, grad, weight, keep,
    mg_out, xt_out, gi_out,
    gbuf, gslot, xslot, pslot, wbuf,
    gsend, grecv, xsend, xrecv, psend, precv, wsem, lsem,
):
    seq = lax.axis_index("seq")
    core = lax.axis_index("dp")
    z, x = seq // XDIM, seq % XDIM
    slots = zdim * XDIM * 2
    rows, cols = grad.shape
    width = cols // CHUNKS
    feats = weight.shape[0]
    tile = cols // keep.shape[1]
    band_tiles = feats // tile
    zdists = range(1, zdim)

    def slot_of(dz, rx, rc):
        return (dz * XDIM + rx) * 2 + rc

    def peer(dz, rx, rc):
        pz = lax.rem(z + dz, zdim)
        px = x if rx == 0 else 1 - x
        pc = core if rc == 0 else 1 - core
        return pz * XDIM + px, pc

    def devid(dz, rx, rc):
        ps, pc = peer(dz, rx, rc)
        return {"seq": ps, "dp": pc}

    everyone = [(dz, rx, rc) for dz in range(zdim) for rx in range(XDIM) for rc in range(2)]
    others = everyone[1:]

    barrier = pltpu.get_barrier_semaphore()
    near = [(dz, 0, 0) for dz in zdists] + [(0, 1, 0), (0, 0, 1)]
    for who in near:
        pl.semaphore_signal(barrier, inc=1, device_id=devid(*who), device_id_type=MESH)

    def wcopy(q):
        c = pl.ds(q * width, width)
        return pltpu.make_async_copy(weight.at[:, c], wbuf.at[:, c], wsem.at[q])

    def own(q):
        return grad.at[:, pl.ds(q * width, width)]

    my_col = pl.multiple_of((seq * 2 + core) * feats, feats)
    xown = pltpu.make_async_copy(act.at[:, pl.ds(my_col, feats)], xslot.at[0], lsem.at[CHUNKS])
    xown.start()
    gown = [pltpu.make_async_copy(own(q), gslot.at[q, 0], lsem.at[q]) for q in range(CHUNKS)]
    for q in range(CHUNKS):
        gown[q].start()
    for q in range(CHUNKS):
        wcopy(q).start()

    pl.semaphore_wait(barrier, len(near))

    def push(q, src, to, dst_slot, sem):
        pltpu.make_async_remote_copy(
            src_ref=src, dst_ref=gslot.at[q, dst_slot],
            send_sem=gsend, recv_sem=grecv.at[q, sem],
            device_id=devid(*to), device_id_type=MESH,
        ).start()

    def arrived(q, sem, count):
        ref = gslot.at[q, pl.ds(0, count)]
        pltpu.make_async_remote_copy(
            src_ref=ref, dst_ref=ref, send_sem=gsend, recv_sem=grecv.at[q, sem],
            device_id=devid(0, 0, 1), device_id_type=MESH,
        ).wait_recv()

    for q in range(CHUNKS):
        for dz in reversed(zdists):
            push(q, own(q), (dz, 0, 0), slot_of(zdim - dz, 0, 0), zdim - dz)
        push(q, own(q), (0, 1, 0), slot_of(0, 1, 0), zdim)
        push(q, own(q), (0, 0, 1), slot_of(0, 0, 1), 0)

    def xcopy(who):
        ps, pc = peer(*who)
        dz, rx, rc = who
        dst = slot_of((zdim - dz) % zdim, rx, rc)
        col = pl.multiple_of((ps * 2 + pc) * feats, feats)
        return pltpu.make_async_remote_copy(
            src_ref=act.at[:, pl.ds(col, feats)], dst_ref=xslot.at[dst],
            send_sem=xsend, recv_sem=xrecv,
            device_id={"seq": ps, "dp": pc}, device_id_type=MESH,
        )

    def z_stage(q):
        for dz in zdists:
            arrived(q, dz, 1)
            slot = slot_of(dz, 0, 0)
            push(q, gslot.at[q, slot], (0, 1, 0), slot_of(dz, 1, 0), zdim + dz)
            push(q, gslot.at[q, slot], (0, 0, 1), slot_of(dz, 0, 1), 0)

    def x_stage(q):
        for dz in range(zdim):
            arrived(q, zdim + dz, 1)
            push(q, gslot.at[q, slot_of(dz, 1, 0)], (0, 0, 1), slot_of(dz, 1, 1), 0)

    def assemble(q, rc):
        for s in range(rc, slots, 2):
            gbuf[rows * s:rows * (s + 1), q * width:(q + 1) * width] = gslot[q, s]

    def compute(q, acc):
        gown[q].wait()
        assemble(q, 0)
        arrived(q, 0, slots // 2)
        if q == 0:
            for who in others:
                xcopy(who).start()
        assemble(q, 1)
        wcopy(q).wait()

        def step(j, acc):
            off = pl.multiple_of(q * width + j * sub, sub)
            g = gbuf[:, pl.ds(off, sub)]
            parts = []
            for a in range(band_tiles):
                pieces = []
                for t in range(sub // tile):
                    kept = keep[core * band_tiles + a, (q * width) // tile + j * (sub // tile) + t]
                    mask = jnp.full((slots * rows, tile), kept.astype(jnp.float32), jnp.float32)
                    pieces.append(g[:, t * tile:(t + 1) * tile] * mask.astype(jnp.bfloat16))
                parts.append(jnp.concatenate(pieces, axis=1))
            lhs = jnp.concatenate(parts, axis=0)
            mg_out[:, pl.ds(off, sub)] = lhs
            return acc + lax.dot_general(
                lhs, wbuf[:, pl.ds(off, sub)], (((1,), (1,)), ((), ())),
                preferred_element_type=jnp.float32,
            )

        return lax.fori_loop(0, width // sub, step, acc, unroll=True)

    acc = jnp.zeros((band_tiles * slots * rows, feats), jnp.float32)
    for q in range(CHUNKS):
        z_stage(q)
    for t in range(CHUNKS + LAG):
        if t < CHUNKS:
            x_stage(t)
        if t >= LAG:
            acc = compute(t - LAG, acc)

    n = slots * rows
    for s in range(slots):
        for a in range(band_tiles):
            pslot[s, :, a * tile:(a + 1) * tile] = acc[a * n + rows * s:a * n + rows * (s + 1), a * tile:(a + 1) * tile]

    for who in others:
        dz, rx, rc = who
        pltpu.make_async_remote_copy(
            src_ref=pslot.at[slot_of(dz, rx, rc)], dst_ref=gi_out.at[:, pl.ds(my_col, feats)],
            send_sem=psend, recv_sem=precv,
            device_id=devid(*who), device_id_type=MESH,
        ).start()
    mine = pltpu.make_async_copy(pslot.at[0], gi_out.at[:, pl.ds(my_col, feats)], lsem.at[CHUNKS + 1])
    mine.start()

    def all_of(ref, send, recv):
        return pltpu.make_async_remote_copy(
            src_ref=ref, dst_ref=ref, send_sem=send, recv_sem=recv,
            device_id=devid(0, 0, 1), device_id_type=MESH,
        )

    rest = pl.ds(0, slots - 1)
    xown.wait()
    xall = all_of(xslot.at[rest], xsend, xrecv)
    xall.wait_recv()
    panel = jnp.concatenate([xslot[s].astype(jnp.float32) for s in range(slots)], axis=0)
    xt_out[...] = panel.T.astype(jnp.bfloat16)

    xall.wait_send()
    all_of(gslot.at[:, rest], gsend, gsend).wait_send()
    mine.wait()
    pall = all_of(pslot.at[rest], psend, precv)
    pall.wait_send()
    pall.wait_recv()


def weight_kernel(band_tiles, blocks, xt, mg, gi, out, gi_out, buf, sem, gsem):
    feats, cols = out.shape
    tile = feats // band_tiles
    tokens = mg.shape[0] // band_tiles
    width = cols // blocks
    step = 2 * tile if width % (2 * tile) == 0 else width
    last = pltpu.make_async_copy(gi, gi_out, gsem)
    last.start()
    x = xt[...]
    for j in range(blocks):
        for lo in range(j * width, (j + 1) * width, step):
            for a in range(band_tiles):
                buf[a * tile:(a + 1) * tile, lo:lo + step] = jnp.dot(
                    x[a * tile:(a + 1) * tile], mg[a * tokens:(a + 1) * tokens, lo:lo + step],
                    preferred_element_type=jnp.float32,
                )
        c = pl.ds(j * width, width)
        pltpu.make_async_copy(buf.at[:, c], out.at[:, c], sem).start()
    last.wait()
    pltpu.make_async_copy(buf, out, sem).wait()


def fused(activations, grad_out, weight, keep):
    rows, cols = grad_out.shape
    feats = weight.shape[0]
    zdim = lax.axis_size("seq") // XDIM
    slots = zdim * XDIM * 2
    tile = cols // keep.shape[1]
    band_tiles = feats // tile
    width = cols // CHUNKS
    sub = SUB * tile if width % (SUB * tile) == 0 else tile
    hbm = pl.BlockSpec(memory_space=pltpu.HBM)
    vmem = pl.BlockSpec(memory_space=pltpu.VMEM)
    smem = pl.BlockSpec(memory_space=pltpu.SMEM)
    dma = pltpu.SemaphoreType.DMA
    mg, xt, gi = pl.pallas_call(
        functools.partial(gather_kernel, zdim, sub),
        name="gather_input_grad",
        out_shape=(
            pltpu.VMEM((band_tiles * slots * rows, cols), jnp.bfloat16),
            pltpu.VMEM((feats, slots * rows), jnp.bfloat16),
            pltpu.VMEM(activations.shape, jnp.float32),
        ),
        in_specs=[hbm, hbm, hbm, smem],
        out_specs=(vmem, vmem, vmem),
        scratch_shapes=[
            pltpu.VMEM((slots * rows, cols), jnp.bfloat16),
            pltpu.VMEM((CHUNKS, slots, rows, width), jnp.bfloat16),
            pltpu.VMEM((slots, rows, feats), jnp.bfloat16),
            pltpu.VMEM((slots, rows, feats), jnp.float32),
            pltpu.VMEM((feats, cols), jnp.bfloat16),
            dma(()),
            dma((CHUNKS, 2 * zdim)),
            dma(()),
            dma(()),
            dma(()),
            dma(()),
            dma((CHUNKS,)),
            dma((CHUNKS + 2,)),
        ],
        compiler_params=pltpu.CompilerParams(
            collective_id=0, has_side_effects=True, vmem_limit_bytes=VMEM_A
        ),
    )(activations, grad_out, weight, keep)
    blocks = 14 if (cols // tile) % 14 == 0 else 1
    gw, gi = pl.pallas_call(
        functools.partial(weight_kernel, band_tiles, blocks),
        name="weight_grad",
        out_shape=(
            jax.ShapeDtypeStruct((feats, cols), jnp.float32),
            jax.ShapeDtypeStruct(gi.shape, jnp.float32),
        ),
        in_specs=[vmem, vmem, vmem],
        out_specs=(hbm, hbm),
        scratch_shapes=[
            pltpu.VMEM((feats, cols), jnp.float32),
            dma(()),
            dma(()),
        ],
        compiler_params=pltpu.CompilerParams(vmem_limit_bytes=VMEM_B),
    )(xt, mg, gi)
    return gw[None], gi


def general(activations, grad_out, weight_regions, keep_blocks):
    tok_rows = activations.shape[0]
    seq_count = lax.axis_size("seq")
    dp_count = lax.axis_size("dp")
    col_groups = seq_count // ROWG
    band_rows = weight_regions.shape[1]
    region_cols = weight_regions.shape[2]
    region_rows = band_rows * dp_count
    core = lax.axis_index("dp")
    grad_groups = grad_out.reshape(tok_rows, col_groups, region_cols).transpose(1, 0, 2)
    grad_send = jnp.repeat(grad_groups, ROWG, axis=0)
    feature_groups = activations.reshape(tok_rows, ROWG, region_rows).transpose(1, 0, 2)
    feature_send = jnp.tile(feature_groups, (col_groups, 1, 1))
    feature_came = lax.all_to_all(feature_send, "seq", split_axis=0, concat_axis=0, tiled=True)
    grad_came = lax.all_to_all(grad_send, "seq", split_axis=0, concat_axis=0, tiled=True)
    half_rows = seq_count * tok_rows
    features = lax.all_gather(feature_came.reshape(half_rows, region_rows), "dp", axis=0, tiled=True)
    features = lax.dynamic_slice_in_dim(features, core * band_rows, band_rows, 1)
    grads = lax.all_gather(grad_came.reshape(half_rows, region_cols), "dp", axis=0, tiled=True)
    tile_rows = keep_blocks.shape[1] // dp_count
    kept = lax.dynamic_slice_in_dim(keep_blocks[0], core * tile_rows, tile_rows, 0)
    side = band_rows // tile_rows
    mask = jnp.repeat(jnp.repeat(kept, side, axis=0), side, axis=1)
    masked_weight = weight_regions[0] * mask.astype(jnp.bfloat16)
    weight_grad = lax.dot_general(
        features, grads, (((0,), (0,)), ((), ())), preferred_element_type=jnp.float32
    ) * mask.astype(jnp.float32)
    partial_value = lax.dot_general(
        grads, masked_weight, (((1,), (1,)), ((), ())), preferred_element_type=jnp.float32
    )
    bands = partial_value.reshape(dp_count, half_rows, band_rows)
    bands = lax.all_to_all(bands, "dp", split_axis=0, concat_axis=0, tiled=True)
    bands = bands.transpose(1, 0, 2).reshape(seq_count, tok_rows, region_rows)
    came = lax.all_to_all(bands, "seq", split_axis=0, concat_axis=0, tiled=True)
    summed = jnp.sum(came.reshape(col_groups, ROWG, tok_rows, region_rows), axis=0)
    return weight_grad[None], summed.transpose(1, 0, 2).reshape(tok_rows, ROWG * region_rows)


def shards(activations, grad_out, weight_regions, keep_blocks):
    if lax.axis_size("seq") == ROWG and lax.axis_size("dp") == 2:
        return fused(activations, grad_out, weight_regions[0], keep_blocks[0])
    return general(activations, grad_out, weight_regions, keep_blocks)


def solution(mesh):
    in_specs = (
        P(("groups", "seq", "dp"), None),
        P(("groups", "seq", "dp"), None),
        P("seq", "dp", None),
        P("seq", None, None),
    )
    out_specs = (P(("groups", "seq"), "dp", None), P(("groups", "seq", "dp"), None))
    return jax.shard_map(shards, mesh=mesh, in_specs=in_specs, out_specs=out_specs, check_vma=False)
```

```python
import functools

import jax
import jax.numpy as jnp
from jax import lax
from jax.experimental import pallas as pl
from jax.experimental.pallas import tpu as pltpu
from jax.sharding import PartitionSpec as P

ROWG = 8
XDIM = 2
CHUNKS = 4
LAG = 1
SUB = 4
VMEM_A = 56 << 20
VMEM_B = 40 << 20
MESH = pl.DeviceIdType.MESH


def gather_kernel(
    zdim, sub, act, grad, weight, keep,
    mg_out, xt_out, gi_out,
    gbuf, gslot, xslot, pslot, wbuf, wturn,
    gsend, grecv, xsend, xrecv, psend, precv, wsem, lsem,
):
    seq = lax.axis_index("seq")
    core = lax.axis_index("dp")
    z, x = seq // XDIM, seq % XDIM
    slots = zdim * XDIM * 2
    rows, cols = grad.shape
    width = cols // CHUNKS
    feats = weight.shape[0]
    tile = cols // keep.shape[1]
    band_tiles = feats // tile
    zdists = range(1, zdim)
    n = slots * rows

    def slot_of(dz, rx, rc):
        return (dz * XDIM + rx) * 2 + rc

    def peer(dz, rx, rc):
        pz = lax.rem(z + dz, zdim)
        px = x if rx == 0 else 1 - x
        pc = core if rc == 0 else 1 - core
        return pz * XDIM + px, pc

    def devid(dz, rx, rc):
        ps, pc = peer(dz, rx, rc)
        return {"seq": ps, "dp": pc}

    everyone = [(dz, rx, rc) for dz in range(zdim) for rx in range(XDIM) for rc in range(2)]
    others = everyone[1:]

    barrier = pltpu.get_barrier_semaphore()
    near = [(dz, 0, 0) for dz in zdists] + [(0, 1, 0), (0, 0, 1)]
    for who in near:
        pl.semaphore_signal(barrier, inc=1, device_id=devid(*who), device_id_type=MESH)

    def wcopy(q):
        c = pl.ds(q * width, width)
        return pltpu.make_async_copy(weight.at[:, c], wbuf.at[:, c], wsem.at[q])

    def own(q):
        return grad.at[:, pl.ds(q * width, width)]

    my_col = pl.multiple_of((seq * 2 + core) * feats, feats)
    xown = pltpu.make_async_copy(act.at[:, pl.ds(my_col, feats)], xslot.at[0], lsem.at[CHUNKS])
    xown.start()
    gown = [pltpu.make_async_copy(own(q), gslot.at[q, 0], lsem.at[q]) for q in range(CHUNKS)]
    for q in range(CHUNKS):
        gown[q].start()
    for q in range(CHUNKS):
        wcopy(q).start()

    pl.semaphore_wait(barrier, len(near))

    def push(q, src, to, dst_slot, sem):
        pltpu.make_async_remote_copy(
            src_ref=src, dst_ref=gslot.at[q, dst_slot],
            send_sem=gsend, recv_sem=grecv.at[q, sem],
            device_id=devid(*to), device_id_type=MESH,
        ).start()

    def arrived(q, sem, count):
        ref = gslot.at[q, pl.ds(0, count)]
        pltpu.make_async_remote_copy(
            src_ref=ref, dst_ref=ref, send_sem=gsend, recv_sem=grecv.at[q, sem],
            device_id=devid(0, 0, 1), device_id_type=MESH,
        ).wait_recv()

    for q in range(CHUNKS):
        for dz in reversed(zdists):
            push(q, own(q), (dz, 0, 0), slot_of(zdim - dz, 0, 0), zdim - dz)
        push(q, own(q), (0, 1, 0), slot_of(0, 1, 0), zdim)
        push(q, own(q), (0, 0, 1), slot_of(0, 0, 1), 0)

    def xcopy(who):
        ps, pc = peer(*who)
        dz, rx, rc = who
        dst = slot_of((zdim - dz) % zdim, rx, rc)
        col = pl.multiple_of((ps * 2 + pc) * feats, feats)
        return pltpu.make_async_remote_copy(
            src_ref=act.at[:, pl.ds(col, feats)], dst_ref=xslot.at[dst],
            send_sem=xsend, recv_sem=xrecv,
            device_id={"seq": ps, "dp": pc}, device_id_type=MESH,
        )

    def z_stage(q):
        for dz in zdists:
            arrived(q, dz, 1)
            slot = slot_of(dz, 0, 0)
            push(q, gslot.at[q, slot], (0, 1, 0), slot_of(dz, 1, 0), zdim + dz)
            push(q, gslot.at[q, slot], (0, 0, 1), slot_of(dz, 0, 1), 0)

    def x_stage(q):
        for dz in range(zdim):
            arrived(q, zdim + dz, 1)
            push(q, gslot.at[q, slot_of(dz, 1, 0)], (0, 0, 1), slot_of(dz, 1, 1), 0)

    def assemble(q, rc):
        for s in range(rc, slots, 2):
            gbuf[rows * s:rows * (s + 1), q * width:(q + 1) * width] = gslot[q, s]

    def compute(q, acc):
        gown[q].wait()
        assemble(q, 0)
        arrived(q, 0, slots // 2)
        if q == 0:
            for who in others:
                xcopy(who).start()
        assemble(q, 1)
        acc = list(acc)
        for lo in range(q * width, (q + 1) * width, sub):
            g = gbuf[:, lo:lo + sub]
            for a in range(band_tiles):
                pieces = []
                for t in range(sub // tile):
                    kept = keep[core * band_tiles + a, lo // tile + t]
                    mask = jnp.full((slots * rows, tile), kept.astype(jnp.float32), jnp.float32)
                    pieces.append(g[:, t * tile:(t + 1) * tile] * mask.astype(jnp.bfloat16))
                lhs = jnp.concatenate(pieces, axis=1)
                mg_out[a * n:(a + 1) * n, lo:lo + sub] = lhs
                acc[a] += jnp.dot(
                    lhs, wturn[lo:lo + sub, a * tile:(a + 1) * tile], preferred_element_type=jnp.float32
                )
        return acc

    def turn(q):
        wcopy(q).wait()
        for lo in range(q * width, (q + 1) * width, 4 * tile):
            wturn[lo:lo + 4 * tile, :] = wbuf[:, lo:lo + 4 * tile].T

    acc = [jnp.zeros((n, tile), jnp.float32)] * band_tiles
    for q in range(CHUNKS):
        if q == 0:
            turn(0)
            turn(1)
        elif q + 1 < CHUNKS:
            turn(q + 1)
        z_stage(q)
    for t in range(CHUNKS + LAG):
        if t < CHUNKS:
            x_stage(t)
        if t >= LAG:
            acc = compute(t - LAG, acc)

    for s in range(slots):
        for a in range(band_tiles):
            pslot[s, :, a * tile:(a + 1) * tile] = acc[a][rows * s:rows * (s + 1)]

    for who in others:
        dz, rx, rc = who
        pltpu.make_async_remote_copy(
            src_ref=pslot.at[slot_of(dz, rx, rc)], dst_ref=gi_out.at[:, pl.ds(my_col, feats)],
            send_sem=psend, recv_sem=precv,
            device_id=devid(*who), device_id_type=MESH,
        ).start()
    mine = pltpu.make_async_copy(pslot.at[0], gi_out.at[:, pl.ds(my_col, feats)], lsem.at[CHUNKS + 1])
    mine.start()

    def all_of(ref, send, recv):
        return pltpu.make_async_remote_copy(
            src_ref=ref, dst_ref=ref, send_sem=send, recv_sem=recv,
            device_id=devid(0, 0, 1), device_id_type=MESH,
        )

    rest = pl.ds(0, slots - 1)
    xown.wait()
    xall = all_of(xslot.at[rest], xsend, xrecv)
    xall.wait_recv()
    panel = jnp.concatenate([xslot[s].astype(jnp.float32) for s in range(slots)], axis=0)
    xt_out[...] = panel.T.astype(jnp.bfloat16)

    xall.wait_send()
    all_of(gslot.at[:, rest], gsend, gsend).wait_send()
    mine.wait()
    pall = all_of(pslot.at[rest], psend, precv)
    pall.wait_send()
    pall.wait_recv()


def weight_kernel(band_tiles, blocks, xt, mg, gi, out, gi_out, buf, sem, gsem):
    feats, cols = out.shape
    tile = feats // band_tiles
    tokens = mg.shape[0] // band_tiles
    width = cols // blocks
    step = 2 * tile if width % (2 * tile) == 0 else width
    last = pltpu.make_async_copy(gi, gi_out, gsem)
    last.start()
    x = xt[...]
    for j in range(blocks):
        for lo in range(j * width, (j + 1) * width, step):
            for a in range(band_tiles):
                buf[a * tile:(a + 1) * tile, lo:lo + step] = jnp.dot(
                    x[a * tile:(a + 1) * tile], mg[a * tokens:(a + 1) * tokens, lo:lo + step],
                    preferred_element_type=jnp.float32,
                )
        c = pl.ds(j * width, width)
        pltpu.make_async_copy(buf.at[:, c], out.at[:, c], sem).start()
    last.wait()
    pltpu.make_async_copy(buf, out, sem).wait()


def fused(activations, grad_out, weight, keep):
    rows, cols = grad_out.shape
    feats = weight.shape[0]
    zdim = lax.axis_size("seq") // XDIM
    slots = zdim * XDIM * 2
    tile = cols // keep.shape[1]
    band_tiles = feats // tile
    width = cols // CHUNKS
    sub = SUB * tile if width % (SUB * tile) == 0 else tile
    hbm = pl.BlockSpec(memory_space=pltpu.HBM)
    vmem = pl.BlockSpec(memory_space=pltpu.VMEM)
    smem = pl.BlockSpec(memory_space=pltpu.SMEM)
    dma = pltpu.SemaphoreType.DMA
    mg, xt, gi = pl.pallas_call(
        functools.partial(gather_kernel, zdim, sub),
        name="gather_input_grad",
        out_shape=(
            pltpu.VMEM((band_tiles * slots * rows, cols), jnp.bfloat16),
            pltpu.VMEM((feats, slots * rows), jnp.bfloat16),
            pltpu.VMEM(activations.shape, jnp.float32),
        ),
        in_specs=[hbm, hbm, hbm, smem],
        out_specs=(vmem, vmem, vmem),
        scratch_shapes=[
            pltpu.VMEM((slots * rows, cols), jnp.bfloat16),
            pltpu.VMEM((CHUNKS, slots, rows, width), jnp.bfloat16),
            pltpu.VMEM((slots, rows, feats), jnp.bfloat16),
            pltpu.VMEM((slots, rows, feats), jnp.float32),
            pltpu.VMEM((feats, cols), jnp.bfloat16),
            pltpu.VMEM((cols, feats), jnp.bfloat16),
            dma(()),
            dma((CHUNKS, 2 * zdim)),
            dma(()),
            dma(()),
            dma(()),
            dma(()),
            dma((CHUNKS,)),
            dma((CHUNKS + 2,)),
        ],
        compiler_params=pltpu.CompilerParams(
            collective_id=0, has_side_effects=True, vmem_limit_bytes=VMEM_A
        ),
    )(activations, grad_out, weight, keep)
    blocks = 14 if (cols // tile) % 14 == 0 else 1
    gw, gi = pl.pallas_call(
        functools.partial(weight_kernel, band_tiles, blocks),
        name="weight_grad",
        out_shape=(
            jax.ShapeDtypeStruct((feats, cols), jnp.float32),
            jax.ShapeDtypeStruct(gi.shape, jnp.float32),
        ),
        in_specs=[vmem, vmem, vmem],
        out_specs=(hbm, hbm),
        scratch_shapes=[
            pltpu.VMEM((feats, cols), jnp.float32),
            dma(()),
            dma(()),
        ],
        compiler_params=pltpu.CompilerParams(vmem_limit_bytes=VMEM_B),
    )(xt, mg, gi)
    return gw[None], gi


def general(activations, grad_out, weight_regions, keep_blocks):
    tok_rows = activations.shape[0]
    seq_count = lax.axis_size("seq")
    dp_count = lax.axis_size("dp")
    col_groups = seq_count // ROWG
    band_rows = weight_regions.shape[1]
    region_cols = weight_regions.shape[2]
    region_rows = band_rows * dp_count
    core = lax.axis_index("dp")
    grad_groups = grad_out.reshape(tok_rows, col_groups, region_cols).transpose(1, 0, 2)
    grad_send = jnp.repeat(grad_groups, ROWG, axis=0)
    feature_groups = activations.reshape(tok_rows, ROWG, region_rows).transpose(1, 0, 2)
    feature_send = jnp.tile(feature_groups, (col_groups, 1, 1))
    feature_came = lax.all_to_all(feature_send, "seq", split_axis=0, concat_axis=0, tiled=True)
    grad_came = lax.all_to_all(grad_send, "seq", split_axis=0, concat_axis=0, tiled=True)
    half_rows = seq_count * tok_rows
    features = lax.all_gather(feature_came.reshape(half_rows, region_rows), "dp", axis=0, tiled=True)
    features = lax.dynamic_slice_in_dim(features, core * band_rows, band_rows, 1)
    grads = lax.all_gather(grad_came.reshape(half_rows, region_cols), "dp", axis=0, tiled=True)
    tile_rows = keep_blocks.shape[1] // dp_count
    kept = lax.dynamic_slice_in_dim(keep_blocks[0], core * tile_rows, tile_rows, 0)
    side = band_rows // tile_rows
    mask = jnp.repeat(jnp.repeat(kept, side, axis=0), side, axis=1)
    masked_weight = weight_regions[0] * mask.astype(jnp.bfloat16)
    weight_grad = lax.dot_general(
        features, grads, (((0,), (0,)), ((), ())), preferred_element_type=jnp.float32
    ) * mask.astype(jnp.float32)
    partial_value = lax.dot_general(
        grads, masked_weight, (((1,), (1,)), ((), ())), preferred_element_type=jnp.float32
    )
    bands = partial_value.reshape(dp_count, half_rows, band_rows)
    bands = lax.all_to_all(bands, "dp", split_axis=0, concat_axis=0, tiled=True)
    bands = bands.transpose(1, 0, 2).reshape(seq_count, tok_rows, region_rows)
    came = lax.all_to_all(bands, "seq", split_axis=0, concat_axis=0, tiled=True)
    summed = jnp.sum(came.reshape(col_groups, ROWG, tok_rows, region_rows), axis=0)
    return weight_grad[None], summed.transpose(1, 0, 2).reshape(tok_rows, ROWG * region_rows)


def shards(activations, grad_out, weight_regions, keep_blocks):
    if lax.axis_size("seq") == ROWG and lax.axis_size("dp") == 2:
        return fused(activations, grad_out, weight_regions[0], keep_blocks[0])
    return general(activations, grad_out, weight_regions, keep_blocks)


def solution(mesh):
    in_specs = (
        P(("groups", "seq", "dp"), None),
        P(("groups", "seq", "dp"), None),
        P("seq", "dp", None),
        P("seq", None, None),
    )
    out_specs = (P(("groups", "seq"), "dp", None), P(("groups", "seq", "dp"), None))
    return jax.shard_map(shards, mesh=mesh, in_specs=in_specs, out_specs=out_specs, check_vma=False)
```
